32 devices in a mesh: ctx: 8 (over y, x, core), grp: 4 (over z).
Axes of the slice: x: 2, y: 2, z: 4, core: 2. Of those that a mesh axis runs over, the one named last changes fastest.
Arguments:
- window_states: bfloat16 [4, 64, 8192], P('grp'), may hold values from -6 to 6
- query_weight: bfloat16 [8192, 8192], P('grp', 'ctx'), may hold values from -0.0625 to 0.0625
- cache_keys: bfloat16 [4, 4096, 1024], P('grp', 'ctx'), may hold values from -65 to 65
- cache_values: bfloat16 [4, 4096, 1024], P('grp', 'ctx'), may hold values from -6 to 6
- kept_blocks: int32 [4, 8, 8], P('grp', None, 'ctx'), may hold values from 0 to 31, as said below
- retained_block_count: int32 [4, 8, 8], P('grp', None, 'ctx'), may hold values from 0 to 1, as said below
- decode_queries: bfloat16 [4, 4, 8, 8192], P('grp', None, 'ctx'), may hold values from -9 to 9
- tail_keys: bfloat16 [4, 8, 64, 1024], P('grp', 'ctx'), may hold values from -6 to 6
- tail_values: bfloat16 [4, 8, 64, 1024], P('grp', 'ctx'), may hold values from -6 to 6
- row_lengths: int32 [4, 8], P('grp', 'ctx'), may hold values from 2 to 61, as said below
Outputs:
- pooled_votes: float32 [4, 8, 4096], P('grp', None, 'ctx')
- decode_out: bfloat16 [4, 4, 8, 8192], P('grp', None, 'ctx')
The draws below stay inside these ranges and needn't reach their ends.
Inputs may be any that keep to these rules, and one draw needn't show every extreme that they name: `kept_blocks`: for key head k, entry c names one block held by ctx index c, that is one of the blocks c * 4 to c * 4 + 3; it is kept only if retained_block_count[g, k, c] is 1. `retained_block_count`: in every request some device holds 1 kept blocks for every key head. `row_lengths`: 61 is reached in every request.
All inputs are finite; a program needn't handle non-finite values.
Results may differ from the reference program's by a relative error of at most 0.0019.
Values may be sent and summed in bfloat16 or wider, within the bound.
No kernel may reach another device: no remote copies, remote signals or barrier semaphores. Data moves between devices by JAX's collectives and lax.ppermute only.
A program may use at most 128 MiB of HBM per device.

```python
import math
import jax
import jax.numpy as jnp
from jax import lax

D = 8192
H = 64
KEY_HEADS = 8
HEAD_DIMENSION = 128
CTX_DEV = 512
WIN = 64
BLOCK_POSITIONS = 128
POOL = 7
STEPS = 4
TAIL = 61
REQUEST_COUNT = 4
CTX = 4096
DROWS = 8
LBLK = 4
NBLK = 32
KEPT_LIMIT = 1
SLOT_COUNT = 8
TAILMAX = 64


def device_order(order_key):
    return jax.random.permutation(order_key, CTX // CTX_DEV)


def kept_plan(key):
    ctx_count = CTX // CTX_DEV
    hot_total = max(1, ctx_count // 8)
    orders = jax.vmap(device_order)(jax.random.split(jax.random.fold_in(key, 11), REQUEST_COUNT))
    hot_mask = jnp.any(orders[:, :hot_total, None] == jnp.arange(ctx_count)[None, None, :], axis=1)
    sparse = jnp.minimum(jax.random.randint(jax.random.fold_in(key, 12), (REQUEST_COUNT, KEY_HEADS, ctx_count), 0, 4), KEPT_LIMIT)
    counts = jnp.where(hot_mask[:, None, :], KEPT_LIMIT, sparse)
    ranking = jax.random.randint(jax.random.fold_in(key, 13), (REQUEST_COUNT, KEY_HEADS, ctx_count, LBLK), 0, 2 ** 20) * LBLK + jnp.arange(LBLK)
    picked = jnp.argsort(ranking, axis=-1)[..., :KEPT_LIMIT]
    blocks = picked + (jnp.arange(ctx_count) * LBLK)[None, None, :, None]
    return (blocks.reshape(REQUEST_COUNT, KEY_HEADS, ctx_count * KEPT_LIMIT).astype(jnp.int32), counts.astype(jnp.int32))


def draw_kept_blocks(key, part):
    return kept_plan(key)[0]


def draw_retained_block_count(key, part):
    return kept_plan(key)[1]


def draw_row_lengths(key, part):
    lengths = jax.random.randint(jax.random.fold_in(key, 21), (REQUEST_COUNT, DROWS), 2, TAIL + 1)
    longest = jax.random.randint(jax.random.fold_in(key, 22), (REQUEST_COUNT, 1), 0, DROWS)
    return jnp.where(jnp.arange(DROWS)[None, :] == longest, TAIL, lengths).astype(jnp.int32)


def draw_cache_keys(key, part):
    shape_all = (REQUEST_COUNT, CTX, KEY_HEADS * HEAD_DIMENSION)
    growth = 1.0 + 0.8 * jnp.arange(CTX).astype(jnp.float32) / CTX
    base_draw = jnp.clip(jax.random.normal(key, shape_all, jnp.float32), -6.0, 6.0)
    base_draw = base_draw * growth[None, :, None]
    return base_draw.astype(jnp.bfloat16)


def draw_decode_queries(key, part):
    shape_all = (REQUEST_COUNT, STEPS, DROWS, H * HEAD_DIMENSION)
    base_draw = jnp.clip(jax.random.normal(key, shape_all, jnp.float32), -6.0, 6.0)
    return base_draw.astype(jnp.bfloat16)


def draw_tail_keys(key, part):
    shape_all = (REQUEST_COUNT, DROWS, TAILMAX, KEY_HEADS * HEAD_DIMENSION)
    base_draw = jnp.clip(jax.random.normal(key, shape_all, jnp.float32), -6.0, 6.0)
    return base_draw.astype(jnp.bfloat16)


def block_scale(key, dims, cuts, smallest, high):
    def one(dim, parts):
        heights = jax.random.uniform(jax.random.fold_in(jax.random.fold_in(key, 6), dim), (parts,), jnp.float32, smallest / len(cuts), high / len(cuts))
        return jnp.repeat(jnp.exp(heights), dims[dim] // parts).reshape((-1,) + (1,) * (len(dims) - dim - 1))

    factor_of = one(*cuts[0])
    for cut in cuts[1:]:
        factor_of = factor_of * one(*cut)
    return factor_of


def noise(own_key, shape, spread, reach, cuts=(), dtype=jnp.bfloat16):
    factor_of = block_scale(own_key, shape, cuts, -0.22, 0.18) if cuts else 1.0
    result = jax.random.normal(own_key, shape, jnp.float32) * spread * factor_of
    return jnp.minimum(jnp.maximum(result, -reach), reach).astype(dtype)


def setup_inputs(seed: int = 0) -> dict:
    key_list = jax.random.split(jax.random.key(seed), 11)
    return {
        "window_states": noise(key_list[0], (REQUEST_COUNT, WIN, D), 1.0, 6.0, ((0, 4),)),
        "query_weight": noise(key_list[1], (D, H * HEAD_DIMENSION), D ** -0.5, 0.0625, ((0, 4), (1, 8))),
        "cache_keys": draw_cache_keys(jax.random.fold_in(key_list[10], 71), 0),
        "cache_values": noise(key_list[3], (REQUEST_COUNT, CTX, KEY_HEADS * HEAD_DIMENSION), 1.0, 6.0, ((0, 4), (1, 8))),
        "kept_blocks": draw_kept_blocks(jax.random.fold_in(key_list[10], 71), 0),
        "retained_block_count": draw_retained_block_count(jax.random.fold_in(key_list[10], 71), 0),
        "decode_queries": draw_decode_queries(jax.random.fold_in(key_list[10], 71), 0),
        "tail_keys": draw_tail_keys(jax.random.fold_in(key_list[10], 71), 0),
        "tail_values": noise(key_list[8], (REQUEST_COUNT, DROWS, TAILMAX, KEY_HEADS * HEAD_DIMENSION), 1.0, 6.0, ((0, 4), (1, 8))),
        "row_lengths": draw_row_lengths(jax.random.fold_in(key_list[10], 71), 0),
    }


def rotary_table(positions, head_size):
    exponent = jnp.arange(0, head_size, 2).astype(jnp.float32) / head_size
    inverse = jnp.power(jnp.float32(500000.0), -exponent)
    wavelength = 2.0 * math.pi / inverse
    smooth = (8192.0 / wavelength - 1.0) / 3.0
    blended = (1.0 - smooth) * inverse / 8.0 + smooth * inverse
    adjusted = jnp.where(wavelength > 8192.0, inverse / 8.0, jnp.where(wavelength < 2048.0, inverse, blended))
    angles = positions[:, None] * adjusted[None, :]
    return (jnp.cos(angles), jnp.sin(angles))

def rotate(vectors, cosine_table, sine_table):
    half_size = vectors.shape[-1] // 2
    leading = vectors[..., :half_size]
    trailing = vectors[..., half_size:]
    cosine_part = cosine_table[:, None, :]
    sine_part = sine_table[:, None, :]
    return jnp.concatenate([leading * cosine_part - trailing * sine_part, trailing * cosine_part + leading * sine_part], axis=-1)

def reference(window_states, query_weight, cache_keys, cache_values, kept_blocks, retained_block_count, decode_queries, tail_keys, tail_values, row_lengths):
    group_size = H // KEY_HEADS
    key_scale = 1.0 / math.sqrt(HEAD_DIMENSION)
    start_pos = CTX - WIN
    positions = (jnp.arange(WIN) + start_pos).astype(jnp.float32)
    cosine_table, sine_table = rotary_table(positions, HEAD_DIMENSION)

    def window_rows(states):
        projected = jnp.dot(states, query_weight, preferred_element_type=jnp.float32)
        turned = rotate(projected.reshape(WIN, H, HEAD_DIMENSION), cosine_table, sine_table)
        return turned.reshape(WIN, H * HEAD_DIMENSION).astype(jnp.bfloat16)
    window_queries = lax.map(window_rows, window_states)
    allowed = jnp.arange(CTX)[None, :] <= (jnp.arange(WIN) + start_pos)[:, None]

    def vote_head(inputs):
        head_queries, key_head_rows = inputs
        scores = jnp.einsum('wgd,td->gwt', head_queries.astype(jnp.float32), key_head_rows.astype(jnp.float32)) * key_scale
        scores = jnp.where(allowed[None], scores, -1e+30)
        peak_value = lax.optimization_barrier(jnp.max(scores, axis=-1, keepdims=True))
        weights = jnp.where(allowed[None], jnp.exp(scores - peak_value), 0.0)
        probability = weights / lax.optimization_barrier(jnp.sum(weights, axis=-1, keepdims=True))
        return lax.optimization_barrier(jnp.sum(probability, axis=(0, 1))) * (CTX / (WIN * group_size))

    def vote_group(inputs):
        group_queries, group_keys = inputs
        per_query = group_queries.reshape(WIN, KEY_HEADS, group_size, HEAD_DIMENSION).transpose(1, 0, 2, 3)
        per_key = group_keys.reshape(CTX, KEY_HEADS, HEAD_DIMENSION).transpose(1, 0, 2)
        return lax.map(vote_head, (per_query, per_key))
    vote_sums = lax.map(vote_group, (window_queries, cache_keys))
    half_width = (POOL - 1) // 2
    padded = jnp.pad(vote_sums, ((0, 0), (0, 0), (half_width, half_width)))
    pooled = padded[:, :, 0:CTX]
    for shift_index in range(1, POOL):
        pooled = pooled + padded[:, :, shift_index:shift_index + CTX]
    pooled_votes = pooled / POOL
    slot_active_mask = (jnp.arange(KEPT_LIMIT)[None, None, None, :] < retained_block_count[:, :, :, None]).reshape(REQUEST_COUNT, KEY_HEADS, SLOT_COUNT)
    steps_range = jnp.arange(STEPS)

    def decode_group(inputs):
        group_queries, group_keys, group_values, group_blocks, group_live, group_tkeys, group_tvalues, group_lengths = inputs
        visible = jnp.arange(TAILMAX)[None, None, :] < group_lengths[None, :, None] + steps_range[:, None, None]
        per_query = group_queries.reshape(STEPS, DROWS, KEY_HEADS, group_size, HEAD_DIMENSION).transpose(2, 0, 1, 3, 4)
        per_key = group_keys.reshape(NBLK, BLOCK_POSITIONS, KEY_HEADS, HEAD_DIMENSION).transpose(2, 0, 1, 3)
        per_value = group_values.reshape(NBLK, BLOCK_POSITIONS, KEY_HEADS, HEAD_DIMENSION).transpose(2, 0, 1, 3)
        tail_key_heads = group_tkeys.reshape(DROWS, TAILMAX, KEY_HEADS, HEAD_DIMENSION).transpose(2, 0, 1, 3)
        tail_value_heads = group_tvalues.reshape(DROWS, TAILMAX, KEY_HEADS, HEAD_DIMENSION).transpose(2, 0, 1, 3)

        def decode_head(head_inputs):
            head_queries, key_head_rows, value_head_rows, per_head_blocks, head_active_mask, head_tkeys, head_tvalues = head_inputs
            selected_keys = key_head_rows[per_head_blocks.astype(jnp.int32)].reshape(SLOT_COUNT * BLOCK_POSITIONS, HEAD_DIMENSION).astype(jnp.float32)
            selected_values = value_head_rows[per_head_blocks.astype(jnp.int32)].reshape(SLOT_COUNT * BLOCK_POSITIONS, HEAD_DIMENSION).astype(jnp.float32)
            key_active_mask = jnp.repeat(head_active_mask, BLOCK_POSITIONS, total_repeat_length=SLOT_COUNT * BLOCK_POSITIONS)
            query_float = head_queries.astype(jnp.float32)
            cache_scores = jnp.einsum('srgd,td->srgt', query_float, selected_keys) * key_scale
            cache_scores = jnp.where(key_active_mask, cache_scores, -1e+30)
            tail_scores = jnp.einsum('srgd,rjd->srgj', query_float, head_tkeys.astype(jnp.float32)) * key_scale
            tail_scores = jnp.where(visible[:, :, None, :], tail_scores, -1e+30)
            peak_value = jnp.maximum(lax.optimization_barrier(jnp.max(cache_scores, axis=-1)), lax.optimization_barrier(jnp.max(tail_scores, axis=-1)))[..., None]
            cache_weights = jnp.where(key_active_mask, jnp.exp(cache_scores - peak_value), 0.0)
            tail_weights = jnp.where(visible[:, :, None, :], jnp.exp(tail_scores - peak_value), 0.0)
            numerator = jnp.einsum('srgt,td->srgd', cache_weights, selected_values, precision=lax.Precision.HIGHEST)
            numerator = numerator + jnp.einsum('srgj,rjd->srgd', tail_weights, head_tvalues.astype(jnp.float32), precision=lax.Precision.HIGHEST)
            denominator = lax.optimization_barrier(jnp.sum(cache_weights, axis=-1)) + lax.optimization_barrier(jnp.sum(tail_weights, axis=-1))
            return numerator / denominator[..., None]
        per_head = lax.map(decode_head, (per_query, per_key, per_value, group_blocks, group_live, tail_key_heads, tail_value_heads))
        return per_head.transpose(1, 2, 0, 3, 4).reshape(STEPS, DROWS, H * HEAD_DIMENSION).astype(jnp.bfloat16)
    decode_out = lax.map(decode_group, (decode_queries, cache_keys, cache_values, kept_blocks, slot_active_mask, tail_keys, tail_values, row_lengths))
    return (pooled_votes, decode_out)
```

```python
import math

import jax
import jax.numpy as jnp
from jax import lax
from jax.sharding import PartitionSpec as P

KEY_HEADS = 8
HEAD_DIMENSION = 128
BLOCK_POSITIONS = 128
POOL = 7


def rotary_table(positions, head_size):
    exponent = jnp.arange(0, head_size, 2).astype(jnp.float32) / head_size
    inverse = jnp.power(jnp.float32(500000.0), -exponent)
    wavelength = 2.0 * math.pi / inverse
    smooth = (8192.0 / wavelength - 1.0) / 3.0
    blended = (1.0 - smooth) * inverse / 8.0 + smooth * inverse
    adjusted = jnp.where(
        wavelength > 8192.0, inverse / 8.0, jnp.where(wavelength < 2048.0, inverse, blended)
    )
    angles = positions[:, None] * adjusted[None, :]
    return (jnp.cos(angles), jnp.sin(angles))


def rotate(vectors, cosine_table, sine_table):
    half_size = vectors.shape[-1] // 2
    leading = vectors[..., :half_size]
    trailing = vectors[..., half_size:]
    cosine_part = cosine_table[:, None, :]
    sine_part = sine_table[:, None, :]
    return jnp.concatenate(
        [
            leading * cosine_part - trailing * sine_part,
            trailing * cosine_part + leading * sine_part,
        ],
        axis=-1,
    )


def exchange(parts, axis):
    return lax.all_to_all(parts, axis, split_axis=0, concat_axis=0, tiled=True)


def on_device(
    window_states,
    query_weight,
    cache_keys,
    cache_values,
    kept_blocks,
    retained_block_count,
    decode_queries,
    tail_keys,
    tail_values,
    row_lengths,
):
    ctx_count = lax.axis_size("ctx")
    grp_count = lax.axis_size("grp")
    ctx_index = lax.axis_index("ctx")
    states = window_states[0]
    win_rows = states.shape[0]
    depth, local_cols = query_weight.shape
    local_heads = local_cols // HEAD_DIMENSION
    head_total = local_heads * ctx_count
    group_size = head_total // KEY_HEADS
    key_scale = 1.0 / math.sqrt(HEAD_DIMENSION)
    key_head_of = [c * local_heads // group_size for c in range(ctx_count)]
    sharers = group_size // local_heads

    slices = states.reshape(win_rows, grp_count, depth).transpose(1, 0, 2)
    all_slices = exchange(slices, "grp").reshape(grp_count * win_rows, depth)
    partial = jnp.dot(all_slices, query_weight, preferred_element_type=jnp.float32)
    partials = exchange(partial.reshape(grp_count, win_rows, local_cols), "grp")
    projected = jnp.sum(partials, axis=0)

    ctx_local = cache_keys.shape[1]
    total_ctx = ctx_local * ctx_count

    def by_head(rows):
        cells = rows.reshape(rows.shape[0], KEY_HEADS, HEAD_DIMENSION).transpose(1, 0, 2)
        if sharers == 1:
            return cells
        return jnp.repeat(cells, sharers, axis=0)

    keys_out = by_head(cache_keys[0])
    head_keys = exchange(keys_out, "ctx").reshape(total_ctx, HEAD_DIMENSION)

    block_total = ctx_local // BLOCK_POSITIONS
    slots = kept_blocks.shape[2]
    local_blocks = kept_blocks[0] - ctx_index * block_total
    local_counts = retained_block_count[0, :, 0]
    head_range = jnp.arange(KEY_HEADS)

    def kept_rows(rows):
        cells = rows.reshape(block_total, BLOCK_POSITIONS, KEY_HEADS, HEAD_DIMENSION)
        picked = cells[local_blocks, :, head_range[:, None], :]
        picked = picked.reshape(KEY_HEADS, slots * BLOCK_POSITIONS, HEAD_DIMENSION)
        return jnp.repeat(picked, sharers, axis=0) if sharers > 1 else picked

    steps = decode_queries.shape[1]
    rows_local = decode_queries.shape[2]
    tail_len = tail_keys.shape[2]
    own_queries = (
        decode_queries[0]
        .reshape(steps, rows_local, ctx_count, local_heads, HEAD_DIMENSION)
        .transpose(2, 1, 0, 3, 4)
        .reshape(ctx_count, rows_local * steps * local_heads, HEAD_DIMENSION)
    )
    tails = [by_head(t[0].reshape(rows_local * tail_len, -1)) for t in (tail_keys, tail_values)]
    counts_out = jnp.repeat(local_counts, sharers)[:, None]
    lengths_out = jnp.broadcast_to(row_lengths[0][None, :], (ctx_count, rows_local))
    notes = jnp.concatenate([counts_out, lengths_out], axis=1).astype(jnp.bfloat16)
    notes = jnp.pad(notes, ((0, 0), (0, HEAD_DIMENSION - notes.shape[1])))[:, None, :]
    notes = jnp.pad(notes, ((0, 0), (0, 15), (0, 0)))
    pieces = [kept_rows(cache_keys[0]), kept_rows(cache_values[0]), own_queries] + tails + [notes]
    sizes = [p.shape[1] for p in pieces]
    arrived = exchange(jnp.concatenate(pieces, axis=1), "ctx")
    starts = [sum(sizes[:i]) for i in range(len(sizes))]
    got = [arrived[:, s : s + n] for s, n in zip(starts, sizes)]
    kept_keys = got[0].reshape(-1, HEAD_DIMENSION)
    kept_values = got[1].reshape(-1, HEAD_DIMENSION)
    rows_all = ctx_count * rows_local
    queries = got[2].reshape(rows_all, steps * local_heads, HEAD_DIMENSION)
    row_keys = got[3].reshape(rows_all, tail_len, HEAD_DIMENSION)
    row_values = got[4].reshape(rows_all, tail_len, HEAD_DIMENSION)
    all_counts = got[5][:, 0, 0].astype(jnp.int32)
    all_lengths = got[5][:, 0, 1 : 1 + rows_local].astype(jnp.int32).reshape(rows_all)

    live = (jnp.arange(slots)[None, :] < all_counts[:, None]).reshape(-1)
    live = jnp.repeat(live, BLOCK_POSITIONS)[None, None, :]
    cache_scores = (
        jnp.einsum("rqd,td->rqt", queries, kept_keys, preferred_element_type=jnp.float32)
        * key_scale
    )
    cache_scores = jnp.where(live, cache_scores, -1e30)
    step_of = jnp.arange(steps * local_heads) // local_heads
    visible = (
        jnp.arange(tail_len)[None, None, :] < all_lengths[:, None, None] + step_of[None, :, None]
    )
    tail_scores = (
        jnp.einsum("rqd,rjd->rqj", queries, row_keys, preferred_element_type=jnp.float32)
        * key_scale
    )
    tail_scores = jnp.where(visible, tail_scores, -1e30)
    peak = jnp.maximum(
        jnp.max(cache_scores, axis=-1, keepdims=True), jnp.max(tail_scores, axis=-1, keepdims=True)
    )
    cache_weights = jnp.where(live, jnp.exp(cache_scores - peak), 0.0)
    tail_weights = jnp.where(visible, jnp.exp(tail_scores - peak), 0.0)
    numerator = jnp.einsum(
        "rqt,td->rqd",
        cache_weights,
        kept_values.astype(jnp.float32),
        precision=lax.Precision.HIGHEST,
    ) + jnp.einsum(
        "rqj,rjd->rqd",
        tail_weights,
        row_values.astype(jnp.float32),
        precision=lax.Precision.HIGHEST,
    )
    denominator = jnp.sum(cache_weights, axis=-1) + jnp.sum(tail_weights, axis=-1)
    decoded = (numerator / denominator[..., None]).astype(jnp.bfloat16)
    decoded = exchange(
        decoded.reshape(ctx_count, rows_local * steps, local_heads * HEAD_DIMENSION), "ctx"
    )
    decode_out = (
        decoded.reshape(ctx_count, rows_local, steps, local_heads * HEAD_DIMENSION)
        .transpose(2, 1, 0, 3)
        .reshape(1, steps, rows_local, head_total * HEAD_DIMENSION)
    )

    start_pos = total_ctx - win_rows
    positions = (jnp.arange(win_rows) + start_pos).astype(jnp.float32)
    cosine_table, sine_table = rotary_table(positions, HEAD_DIMENSION)
    turned = rotate(
        projected.reshape(win_rows, local_heads, HEAD_DIMENSION), cosine_table, sine_table
    ).astype(jnp.bfloat16)
    allowed = jnp.arange(total_ctx)[None, :] <= (start_pos + jnp.arange(win_rows))[:, None]
    scores = (
        jnp.einsum("wgd,td->gwt", turned, head_keys, preferred_element_type=jnp.float32)
        * key_scale
    )
    scores = jnp.where(allowed[None], scores, -1e30)
    row_max = jnp.max(scores, axis=-1, keepdims=True)
    weights = jnp.where(allowed[None], jnp.exp(scores - row_max), 0.0)
    row_sum = jnp.sum(weights, axis=-1, keepdims=True)
    votes = jnp.sum(weights / row_sum, axis=(0, 1)) * (total_ctx / (win_rows * group_size))
    half_width = (POOL - 1) // 2
    padded = jnp.pad(votes, (half_width, half_width))
    pooled = padded[0:total_ctx]
    for shift_index in range(1, POOL):
        pooled = pooled + padded[shift_index : shift_index + total_ctx]
    shares = exchange((pooled / POOL).reshape(ctx_count, 1, ctx_local), "ctx")
    pooled_votes = jnp.sum(shares.reshape(KEY_HEADS, sharers, ctx_local), axis=1)[None]
    return (pooled_votes, decode_out)


def solution(mesh):
    placed = (
        P("grp", None, None),
        P("grp", "ctx"),
        P("grp", "ctx", None),
        P("grp", "ctx", None),
        P("grp", None, "ctx"),
        P("grp", None, "ctx"),
        P("grp", None, "ctx", None),
        P("grp", "ctx", None, None),
        P("grp", "ctx", None, None),
        P("grp", "ctx"),
    )
    return jax.shard_map(
        on_device,
        mesh=mesh,
        in_specs=placed,
        out_specs=(P("grp", None, "ctx"), P("grp", None, "ctx", None)),
        check_vma=False,
    )
```

```python
import functools
import math

import jax
import jax.numpy as jnp
from jax import lax
from jax.experimental import pallas as pl
from jax.experimental.pallas import tpu as pltpu
from jax.sharding import PartitionSpec as P

KEY_HEADS = 8
HEAD_DIMENSION = 128
BLOCK_POSITIONS = 128
POOL = 7
LANES = 128
NOTE_ROWS = 16


def rotary_table(positions, head_size):
    exponent = jnp.arange(0, head_size, 2).astype(jnp.float32) / head_size
    inverse = jnp.power(jnp.float32(500000.0), -exponent)
    wavelength = 2.0 * math.pi / inverse
    smooth = (8192.0 / wavelength - 1.0) / 3.0
    blended = (1.0 - smooth) * inverse / 8.0 + smooth * inverse
    adjusted = jnp.where(
        wavelength > 8192.0, inverse / 8.0, jnp.where(wavelength < 2048.0, inverse, blended)
    )
    angles = positions[:, None] * adjusted[None, :]
    return (jnp.cos(angles), jnp.sin(angles))


def swap(value, axis, mask):
    count = lax.axis_size(axis)
    return lax.ppermute(value, axis, [(i, i ^ mask) for i in range(count)])


def vmem():
    return pl.BlockSpec(memory_space=pltpu.VMEM)


def smem():
    return pl.BlockSpec(memory_space=pltpu.SMEM)


def round_up(value, step):
    return (value + step - 1) // step * step


def dot_t(left, right):
    return lax.dot_general(
        left, right, (((1,), (1,)), ((), ())), preferred_element_type=jnp.float32
    )


def dot_exact(left, right):
    total = None
    for _ in range(3):
        part = left.astype(jnp.bfloat16)
        left = left - part.astype(jnp.float32)
        term = jnp.dot(part, right, preferred_element_type=jnp.float32)
        total = term if total is None else total + term
    return total


def payload_kernel(
    layout, me_ref, blocks_ref, counts_ref, lengths_ref, keys_ref, values_ref, query_ref,
    tail_k_ref, tail_v_ref, *out_refs
):
    ctx_local, steps, local_heads, group_size, block_total, tail_len = layout["dims"]
    at = layout["at"]
    me = me_ref[0]
    lane = lax.broadcasted_iota(jnp.int32, (NOTE_ROWS, LANES), 1)
    for mask, out in enumerate(out_refs):
        dest = me ^ mask
        head = dest * local_heads // group_size
        columns = pl.ds(pl.multiple_of(head * HEAD_DIMENSION, HEAD_DIMENSION), HEAD_DIMENSION)
        out[0:ctx_local, :] = keys_ref[:, columns]
        block = jnp.clip(blocks_ref[head] - me * block_total, 0, block_total - 1)
        rows = pl.ds(pl.multiple_of(block * BLOCK_POSITIONS, BLOCK_POSITIONS), BLOCK_POSITIONS)
        out[at["values"] : at["values"] + BLOCK_POSITIONS, :] = values_ref[rows, columns]
        parts = []
        for g in range(local_heads):
            start = (dest * local_heads + g) * HEAD_DIMENSION
            cols = pl.ds(pl.multiple_of(start, HEAD_DIMENSION), HEAD_DIMENSION)
            parts.append(query_ref[:, cols].astype(jnp.float32))
        queries = jnp.concatenate(parts, axis=0)
        pad = at["tail_k"] - at["queries"] - steps * local_heads
        if pad:
            queries = jnp.concatenate(
                [queries, jnp.zeros((pad, HEAD_DIMENSION), jnp.float32)], axis=0
            )
        out[at["queries"] : at["tail_k"], :] = queries.astype(jnp.bfloat16)
        out[at["tail_k"] : at["tail_k"] + tail_len, :] = tail_k_ref[:, columns]
        out[at["tail_v"] : at["tail_v"] + tail_len, :] = tail_v_ref[:, columns]
        count = counts_ref[head].astype(jnp.float32)
        notes = jnp.where(
            lane == 0,
            count,
            jnp.where(
                lane == 1,
                block.astype(jnp.float32),
                jnp.where(lane == 2, lengths_ref[0].astype(jnp.float32), 0.0),
            ),
        )
        out[at["notes"] : at["notes"] + NOTE_ROWS, :] = notes.astype(jnp.bfloat16)


def decode_kernel(layout, me_ref, *refs):
    ctx_local, steps, local_heads, group_size, block_total, tail_len = layout["dims"]
    at = layout["at"]
    scale = layout["scale"]
    pieces, out_ref = refs[:-1], refs[-1]
    me = me_ref[0]
    span = steps * local_heads
    kept_k, kept_v, queries, bias, tails = [], [], [], [], []
    for piece in pieces:
        notes = piece[at["notes"] : at["notes"] + NOTE_ROWS, :].astype(jnp.float32)
        block = notes[0:1, 1:2]
        bias.append(jnp.where(notes[0:1, 0:1] > 0.5, 0.0, -1e30))
        chosen = None
        for b in range(block_total):
            cell = piece[b * BLOCK_POSITIONS : (b + 1) * BLOCK_POSITIONS, :].astype(jnp.float32)
            term = cell * jnp.where(block == float(b), 1.0, 0.0)
            chosen = term if chosen is None else chosen + term
        kept_k.append(chosen.astype(jnp.bfloat16))
        kept_v.append(piece[at["values"] : at["values"] + BLOCK_POSITIONS, :])
        own = piece[at["queries"] : at["tail_k"], :]
        if at["tail_k"] - at["queries"] > span:
            own = own.astype(jnp.float32)[:span].astype(jnp.bfloat16)
        queries.append(own)
        score = dot_t(own, piece[at["tail_k"] : at["tail_k"] + tail_len, :]) * scale
        slot = lax.broadcasted_iota(jnp.int32, (span, tail_len), 1)
        step = lax.rem(lax.broadcasted_iota(jnp.int32, (span, tail_len), 0), steps)
        visible = (slot - step).astype(jnp.float32) < notes[0:1, 2:3]
        tails.append(jnp.where(visible, score, -1e30))
    every = jnp.concatenate(queries, axis=0)
    scores = [dot_t(every, k) * scale + b for k, b in zip(kept_k, bias)]
    peak = scores[0]
    for s in scores[1:]:
        peak = jnp.maximum(peak, s)
    peak = jnp.max(peak, axis=1, keepdims=True)
    tail_peak = jnp.concatenate([jnp.max(t, axis=1, keepdims=True) for t in tails], axis=0)
    peak = jnp.maximum(peak, tail_peak)
    weights = [jnp.exp(s - peak) for s in scores]
    total = weights[0]
    for w in weights[1:]:
        total = total + w
    total = jnp.sum(total, axis=1, keepdims=True)
    numerator = dot_exact(jnp.concatenate(weights, axis=1), jnp.concatenate(kept_v, axis=0))
    for mask, piece in enumerate(pieces):
        lo = mask * span
        weight = jnp.exp(tails[mask] - peak[lo : lo + span])
        part = dot_exact(weight, piece[at["tail_v"] : at["tail_v"] + tail_len, :])
        top = numerator[lo : lo + span] + part
        bottom = total[lo : lo + span] + jnp.sum(weight, axis=1, keepdims=True)
        result = top / bottom
        dest = me ^ mask
        for g in range(local_heads):
            out_ref[dest, :, g * HEAD_DIMENSION : (g + 1) * HEAD_DIMENSION] = result[
                g * steps : (g + 1) * steps
            ].astype(jnp.bfloat16)


def votes_kernel(layout, me_ref, projected_ref, cos_ref, sin_ref, *refs):
    ctx_local, steps, local_heads, group_size, block_total, tail_len = layout["dims"]
    count = layout["ctx"]
    scale = layout["scale"]
    win = projected_ref.shape[0]
    pieces, out_ref = refs[:count], refs[count]
    score_ref, sums_ref = refs[count + 1 :]
    me = me_ref[0]
    total_ctx = ctx_local * count
    start_pos = total_ctx - win
    folded = scale * math.log2(math.e)
    edge = ctx_local - LANES
    offset = lax.broadcasted_iota(jnp.int32, (win, LANES), 1) - lax.broadcasted_iota(
        jnp.int32, (win, LANES), 0
    )
    half = HEAD_DIMENSION // 2
    votes = None
    for g in range(local_heads):
        x = projected_ref[:, g * HEAD_DIMENSION : (g + 1) * HEAD_DIMENSION]
        turned = x * cos_ref[...] + jnp.concatenate([x[:, half:], x[:, :half]], axis=1) * sin_ref[...]
        turned = turned.astype(jnp.bfloat16)
        peak = None
        for mask, piece in enumerate(pieces):
            source = me ^ mask
            score = dot_t(turned, piece[0:ctx_local, :])
            last = jnp.where(
                offset <= start_pos - source * ctx_local - edge, score[:, edge:], -1e30
            )
            base = source * ctx_local
            if edge:
                at = pl.ds(pl.multiple_of(base, LANES), edge)
                score_ref[:, at] = score[:, :edge]
            score_ref[:, pl.ds(pl.multiple_of(base + edge, LANES), LANES)] = last
            for c in range(edge // LANES):
                block = score[:, c * LANES : (c + 1) * LANES]
                peak = block if peak is None else jnp.maximum(peak, block)
            peak = last if peak is None else jnp.maximum(peak, last)
        peak = jnp.max(peak, axis=1, keepdims=True) * folded
        weight = jnp.exp2(score_ref[...] * folded - peak)
        share = 1.0 / jnp.sum(weight, axis=1, keepdims=True)
        weight = weight * share
        cells = jnp.sum(weight.reshape(win // 8, 8, total_ctx), axis=0)
        votes = cells if votes is None else votes + cells
    row = jnp.sum(votes, axis=0, keepdims=True) * (total_ctx / (win * group_size))
    sums_ref[:, 0:LANES] = jnp.zeros((1, LANES), jnp.float32)
    sums_ref[:, LANES : LANES + total_ctx] = row
    sums_ref[:, LANES + total_ctx :] = jnp.zeros((1, LANES), jnp.float32)
    pooled = None
    for shift in range(POOL):
        start = LANES - (POOL - 1) // 2 + shift
        term = sums_ref[:, start : start + total_ctx]
        pooled = term if pooled is None else pooled + term
    pooled = pooled / POOL
    for c in range(count):
        out_ref[c] = pooled[:, c * ctx_local : (c + 1) * ctx_local]


def on_device(
    window_states,
    query_weight,
    cache_keys,
    cache_values,
    kept_blocks,
    retained_block_count,
    decode_queries,
    tail_keys,
    tail_values,
    row_lengths,
):
    ctx_count = lax.axis_size("ctx")
    grp_count = lax.axis_size("grp")
    ctx_index = lax.axis_index("ctx")
    grp_index = lax.axis_index("grp")
    states = window_states[0]
    win_rows = states.shape[0]
    depth, local_cols = query_weight.shape
    local_heads = local_cols // HEAD_DIMENSION
    head_total = local_heads * ctx_count
    group_size = head_total // KEY_HEADS
    sharers = group_size // local_heads
    ctx_local = cache_keys.shape[1]
    total_ctx = ctx_local * ctx_count
    steps = decode_queries.shape[1]
    tail_len = tail_keys.shape[2]
    block_total = ctx_local // BLOCK_POSITIONS
    assert decode_queries.shape[2] == 1 and kept_blocks.shape[2] == 1
    at, row = {}, ctx_local
    sizes = (
        ("values", BLOCK_POSITIONS),
        ("queries", round_up(steps * local_heads, 16)),
        ("tail_k", tail_len),
        ("tail_v", tail_len),
        ("notes", NOTE_ROWS),
    )
    for name, size in sizes:
        at[name] = row
        row += size
    layout = {
        "dims": (ctx_local, steps, local_heads, group_size, block_total, tail_len),
        "at": at,
        "scale": 1.0 / math.sqrt(HEAD_DIMENSION),
        "ctx": ctx_count,
    }
    me = ctx_index.astype(jnp.int32).reshape(1)

    part_rows = win_rows // 2
    core = ctx_index % 2
    cells = states.reshape(win_rows, grp_count, depth)
    order = list(range(grp_count - 1, 0, -1))
    fetched = {}
    for mask in order:
        cell = lax.dynamic_slice(
            cells, (core * part_rows, grp_index ^ mask, 0), (part_rows, 1, depth)
        )
        fetched[mask] = swap(cell.reshape(part_rows, depth), "grp", mask)

    payload = pl.pallas_call(
        functools.partial(payload_kernel, layout),
        out_shape=[jax.ShapeDtypeStruct((row, HEAD_DIMENSION), jnp.bfloat16)] * ctx_count,
        in_specs=[smem()] * 4 + [vmem()] * 5,
        out_specs=[vmem()] * ctx_count,
    )(
        me,
        kept_blocks.reshape(KEY_HEADS),
        retained_block_count.reshape(KEY_HEADS),
        row_lengths.reshape(1),
        cache_keys[0],
        cache_values[0],
        decode_queries.reshape(steps, head_total * HEAD_DIMENSION),
        tail_keys[0, 0],
        tail_values[0, 0],
    )
    pieces = [payload[0]] + [swap(payload[m], "ctx", m) for m in range(1, ctx_count)]

    own = lax.dynamic_index_in_dim(cells, grp_index, 1, False)
    projected = jnp.dot(own, query_weight, preferred_element_type=jnp.float32)
    for mask in range(1, grp_count):
        mine = fetched[mask]
        other = swap(mine, "ctx", 1)
        both = jnp.where(
            core == 0,
            jnp.concatenate([mine, other], axis=0),
            jnp.concatenate([other, mine], axis=0),
        )
        partial = jnp.dot(both, query_weight, preferred_element_type=jnp.float32)
        back = swap(partial.astype(jnp.float16), "grp", mask)
        projected = projected + back.astype(jnp.float32)

    decoded = pl.pallas_call(
        functools.partial(decode_kernel, layout),
        out_shape=jax.ShapeDtypeStruct((ctx_count, steps, local_cols), jnp.bfloat16),
        in_specs=[smem()] + [vmem()] * ctx_count,
        out_specs=vmem(),
    )(me, *pieces)
    decoded = lax.all_to_all(decoded, "ctx", split_axis=0, concat_axis=0, tiled=True)
    decode_out = decoded.transpose(1, 0, 2).reshape(1, steps, 1, head_total * HEAD_DIMENSION)

    positions = (jnp.arange(win_rows) + (total_ctx - win_rows)).astype(jnp.float32)
    cosine, sine = rotary_table(positions, HEAD_DIMENSION)
    cosine = jnp.concatenate([cosine, cosine], axis=1)
    sine = jnp.concatenate([-sine, sine], axis=1)
    pooled = pl.pallas_call(
        functools.partial(votes_kernel, layout),
        out_shape=jax.ShapeDtypeStruct((ctx_count, 1, ctx_local), jnp.float32),
        in_specs=[smem()] + [vmem()] * (3 + ctx_count),
        out_specs=vmem(),
        scratch_shapes=[
            pltpu.VMEM((win_rows, total_ctx), jnp.float32),
            pltpu.VMEM((1, total_ctx + 2 * LANES), jnp.float32),
        ],
    )(me, projected, cosine, sine, *pieces)
    shares = lax.all_to_all(pooled, "ctx", split_axis=0, concat_axis=0, tiled=True)
    shares = shares.reshape(KEY_HEADS, sharers, ctx_local)
    pooled_votes = (shares[:, 0] if sharers == 1 else jnp.sum(shares, axis=1))[None]
    return (pooled_votes, decode_out)


def solution(mesh):
    placed = (
        P("grp", None, None),
        P("grp", "ctx"),
        P("grp", "ctx", None),
        P("grp", "ctx", None),
        P("grp", None, "ctx"),
        P("grp", None, "ctx"),
        P("grp", None, "ctx", None),
        P("grp", "ctx", None, None),
        P("grp", "ctx", None, None),
        P("grp", "ctx"),
    )
    return jax.shard_map(
        on_device,
        mesh=mesh,
        in_specs=placed,
        out_specs=(P("grp", None, "ctx"), P("grp", None, "ctx", None)),
        check_vma=False,
    )
```

```python
import functools
import math

import jax
import jax.numpy as jnp
from jax import lax
from jax.experimental import pallas as pl
from jax.experimental.pallas import tpu as pltpu
from jax.sharding import PartitionSpec as P


KEY_HEADS = 8
HEAD_DIMENSION = 128
BLOCK_POSITIONS = 128
POOL = 7
LANES = 128
NOTE_ROWS = 16


def rotary_table(positions, head_size):
    exponent = jnp.arange(0, head_size, 2).astype(jnp.float32) / head_size
    inverse = jnp.power(jnp.float32(500000.0), -exponent)
    wavelength = 2.0 * math.pi / inverse
    smooth = (8192.0 / wavelength - 1.0) / 3.0
    blended = (1.0 - smooth) * inverse / 8.0 + smooth * inverse
    adjusted = jnp.where(
        wavelength > 8192.0, inverse / 8.0, jnp.where(wavelength < 2048.0, inverse, blended)
    )
    angles = positions[:, None] * adjusted[None, :]
    return (jnp.cos(angles), jnp.sin(angles))


def swap(value, axis, mask):
    count = lax.axis_size(axis)
    return lax.ppermute(value, axis, [(i, i ^ mask) for i in range(count)])


def vmem():
    return pl.BlockSpec(memory_space=pltpu.VMEM)


def far():
    return pl.BlockSpec(memory_space=pltpu.HBM)


def smem():
    return pl.BlockSpec(memory_space=pltpu.SMEM)


def near(*arrays):
    return [pltpu.with_memory_space_constraint(a, pltpu.VMEM) for a in arrays]


def away(*arrays):
    return [pltpu.with_memory_space_constraint(a, pltpu.HBM) for a in arrays]


def room(mebibytes):
    return pltpu.CompilerParams(vmem_limit_bytes=mebibytes * 1024 * 1024)


def round_up(value, step):
    return (value + step - 1) // step * step


def dot_t(left, right):
    return lax.dot_general(
        left, right, (((1,), (1,)), ((), ())), preferred_element_type=jnp.float32
    )


def dot_exact(left, right):
    total = None
    for _ in range(3):
        part = left.astype(jnp.bfloat16)
        left = left - part.astype(jnp.float32)
        term = jnp.dot(part, right, preferred_element_type=jnp.float32)
        total = term if total is None else total + term
    return total


def fetch_kernel(order, depth, me_ref, group_ref, states_ref, *refs):
    outs, sems = refs[:-1], refs[-1]
    part_rows = outs[0].shape[0]
    start = pl.multiple_of(lax.rem(me_ref[0], 2) * part_rows, part_rows)
    copies = []
    for i, mask in enumerate(order):
        columns = pl.ds(pl.multiple_of((group_ref[0] ^ mask) * depth, LANES), depth)
        source = states_ref.at[pl.ds(start, part_rows), columns]
        copies.append(pltpu.make_async_copy(source, outs[i], sems.at[i]))
    for copy in copies:
        copy.start()
    for copy in copies:
        copy.wait()


def payload_kernel(
    layout, me_ref, blocks_ref, counts_ref, lengths_ref, keys_ref, values_ref, query_ref,
    tail_k_ref, tail_v_ref, *refs
):
    ctx_local, steps, local_heads, group_size, block_total, tail_len = layout["dims"]
    at = layout["at"]
    out_refs, sems = refs[:-1], refs[-1]
    me = me_ref[0]
    lane = lax.broadcasted_iota(jnp.int32, (NOTE_ROWS, LANES), 1)
    copies = []
    for mask, out in enumerate(out_refs):
        head = (me ^ mask) * local_heads // group_size
        columns = pl.ds(pl.multiple_of(head * HEAD_DIMENSION, HEAD_DIMENSION), HEAD_DIMENSION)
        block = jnp.clip(blocks_ref[head] - me * block_total, 0, block_total - 1)
        rows = pl.ds(pl.multiple_of(block * BLOCK_POSITIONS, BLOCK_POSITIONS), BLOCK_POSITIONS)
        moves = (
            (keys_ref.at[:, columns], 0, ctx_local),
            (values_ref.at[rows, columns], at["values"], BLOCK_POSITIONS),
            (tail_k_ref.at[:, columns], at["tail_k"], tail_len),
            (tail_v_ref.at[:, columns], at["tail_v"], tail_len),
        )
        for i, (source, start, size) in enumerate(moves):
            target = out.at[pl.ds(start, size), :]
            copies.append(pltpu.make_async_copy(source, target, sems.at[mask, i]))
            copies[-1].start()
    for mask, out in enumerate(out_refs):
        dest = me ^ mask
        head = dest * local_heads // group_size
        block = jnp.clip(blocks_ref[head] - me * block_total, 0, block_total - 1)
        parts = []
        for g in range(local_heads):
            start = (dest * local_heads + g) * HEAD_DIMENSION
            cols = pl.ds(pl.multiple_of(start, HEAD_DIMENSION), HEAD_DIMENSION)
            parts.append(query_ref[:, cols].astype(jnp.float32))
        queries = jnp.concatenate(parts, axis=0)
        pad = at["tail_k"] - at["queries"] - steps * local_heads
        if pad:
            queries = jnp.concatenate(
                [queries, jnp.zeros((pad, HEAD_DIMENSION), jnp.float32)], axis=0
            )
        out[at["queries"] : at["tail_k"], :] = queries.astype(jnp.bfloat16)
        count = counts_ref[head].astype(jnp.float32)
        notes = jnp.where(
            lane == 0,
            count,
            jnp.where(
                lane == 1,
                block.astype(jnp.float32),
                jnp.where(lane == 2, lengths_ref[0].astype(jnp.float32), 0.0),
            ),
        )
        out[at["notes"] : at["notes"] + NOTE_ROWS, :] = notes.astype(jnp.bfloat16)
    for copy in copies:
        copy.wait()


def decode_kernel(layout, me_ref, *refs):
    _, steps, local_heads, _, block_total, tail_len = layout["dims"]
    at = layout["at"]
    scale = layout["scale"]
    pieces, out_ref = refs[:-1], refs[-1]
    me = me_ref[0]
    span = steps * local_heads
    kept_k, kept_v, queries, bias, tails = [], [], [], [], []
    for piece in pieces:
        notes = piece[at["notes"] : at["notes"] + NOTE_ROWS, :].astype(jnp.float32)
        block = notes[0:1, 1:2]
        bias.append(jnp.where(notes[0:1, 0:1] > 0.5, 0.0, -1e30))
        chosen = None
        for b in range(block_total):
            cell = piece[b * BLOCK_POSITIONS : (b + 1) * BLOCK_POSITIONS, :].astype(jnp.float32)
            term = cell * jnp.where(block == float(b), 1.0, 0.0)
            chosen = term if chosen is None else chosen + term
        kept_k.append(chosen.astype(jnp.bfloat16))
        kept_v.append(piece[at["values"] : at["values"] + BLOCK_POSITIONS, :])
        own = piece[at["queries"] : at["tail_k"], :]
        if at["tail_k"] - at["queries"] > span:
            own = own.astype(jnp.float32)[:span].astype(jnp.bfloat16)
        queries.append(own)
        score = dot_t(own, piece[at["tail_k"] : at["tail_k"] + tail_len, :]) * scale
        slot = lax.broadcasted_iota(jnp.int32, (span, tail_len), 1)
        step = lax.rem(lax.broadcasted_iota(jnp.int32, (span, tail_len), 0), steps)
        visible = (slot - step).astype(jnp.float32) < notes[0:1, 2:3]
        tails.append(jnp.where(visible, score, -1e30))
    every = jnp.concatenate(queries, axis=0)
    scores = [dot_t(every, k) * scale + b for k, b in zip(kept_k, bias)]
    peak = scores[0]
    for s in scores[1:]:
        peak = jnp.maximum(peak, s)
    peak = jnp.max(peak, axis=1, keepdims=True)
    tail_peak = jnp.concatenate([jnp.max(t, axis=1, keepdims=True) for t in tails], axis=0)
    peak = jnp.maximum(peak, tail_peak)
    weights = [jnp.exp(s - peak) for s in scores]
    total = weights[0]
    for w in weights[1:]:
        total = total + w
    total = jnp.sum(total, axis=1, keepdims=True)
    numerator = dot_exact(jnp.concatenate(weights, axis=1), jnp.concatenate(kept_v, axis=0))
    for mask, piece in enumerate(pieces):
        lo = mask * span
        weight = jnp.exp(tails[mask] - peak[lo : lo + span])
        part = dot_exact(weight, piece[at["tail_v"] : at["tail_v"] + tail_len, :])
        top = numerator[lo : lo + span] + part
        bottom = total[lo : lo + span] + jnp.sum(weight, axis=1, keepdims=True)
        result = top / bottom
        dest = me ^ mask
        for g in range(local_heads):
            out_ref[dest, :, g * HEAD_DIMENSION : (g + 1) * HEAD_DIMENSION] = result[
                g * steps : (g + 1) * steps
            ].astype(jnp.bfloat16)


def votes_kernel(layout, me_ref, projected_ref, cos_ref, sin_ref, *refs):
    ctx_local, _, local_heads, group_size, _, _ = layout["dims"]
    count = layout["ctx"]
    win = projected_ref.shape[0]
    pieces, out_ref = refs[:count], refs[count + 1]
    query_ref, score_ref, peak_ref, sums_ref = refs[count + 2 :]
    me = me_ref[0]
    total_ctx = ctx_local * count
    start_pos = total_ctx - win
    folded = layout["scale"] * math.log2(math.e)
    rows = win * local_heads
    width = 2 * LANES
    half = HEAD_DIMENSION // 2
    for g in range(local_heads):
        x = projected_ref[:, g * HEAD_DIMENSION : (g + 1) * HEAD_DIMENSION]
        turned = jnp.concatenate([x[:, half:], x[:, :half]], axis=1)
        turned = x * cos_ref[...] + turned * sin_ref[...]
        query_ref[g * win : (g + 1) * win, :] = turned.astype(jnp.bfloat16)
    offset = lax.broadcasted_iota(jnp.int32, (win, LANES), 1) - lax.broadcasted_iota(
        jnp.int32, (win, LANES), 0
    )
    for mask, piece in enumerate(pieces):
        base = (me ^ mask) * ctx_local
        for c in range(0, ctx_local, width):
            score = dot_t(query_ref[...], piece[c : c + width, :])
            if c + width == ctx_local:
                seen = offset <= start_pos - base - (ctx_local - LANES)
                last = score[:, LANES:].reshape(local_heads, win, LANES)
                last = jnp.where(seen[None], last, -1e30).reshape(rows, LANES)
                score = jnp.concatenate([score[:, :LANES], last], axis=1)
            score_ref[:, pl.ds(pl.multiple_of(base + c, LANES), width)] = score
            top = jnp.maximum(score[:, :LANES], score[:, LANES:])
            first = mask == 0 and c == 0
            peak_ref[...] = top if first else jnp.maximum(peak_ref[...], top)
    votes = None
    for g in range(local_heads):
        at = slice(g * win, (g + 1) * win)
        peak = jnp.max(peak_ref[at, :], axis=1, keepdims=True) * folded
        weight = jnp.exp2(score_ref[at, :] * folded - peak)
        share = 1.0 / jnp.sum(weight, axis=1, keepdims=True)
        weight = weight * share
        cells = jnp.sum(weight.reshape(win // 8, 8, total_ctx), axis=0)
        votes = cells if votes is None else votes + cells
    row = jnp.sum(votes, axis=0, keepdims=True) * (total_ctx / (win * group_size))
    sums_ref[:, 0:LANES] = jnp.zeros((1, LANES), jnp.float32)
    sums_ref[:, LANES : LANES + total_ctx] = row
    sums_ref[:, LANES + total_ctx :] = jnp.zeros((1, LANES), jnp.float32)
    pooled = None
    for shift in range(POOL):
        start = LANES - (POOL - 1) // 2 + shift
        term = sums_ref[:, start : start + total_ctx]
        pooled = term if pooled is None else pooled + term
    pooled = pooled / POOL
    for c in range(count):
        out_ref[c] = pooled[:, c * ctx_local : (c + 1) * ctx_local]


def on_device(
    window_states,
    query_weight,
    cache_keys,
    cache_values,
    kept_blocks,
    retained_block_count,
    decode_queries,
    tail_keys,
    tail_values,
    row_lengths,
):
    ctx_count = lax.axis_size("ctx")
    grp_count = lax.axis_size("grp")
    ctx_index = lax.axis_index("ctx")
    grp_index = lax.axis_index("grp")
    states = window_states[0]
    win_rows = states.shape[0]
    depth, local_cols = query_weight.shape
    local_heads = local_cols // HEAD_DIMENSION
    head_total = local_heads * ctx_count
    group_size = head_total // KEY_HEADS
    sharers = group_size // local_heads
    ctx_local = cache_keys.shape[1]
    total_ctx = ctx_local * ctx_count
    steps = decode_queries.shape[1]
    tail_len = tail_keys.shape[2]
    block_total = ctx_local // BLOCK_POSITIONS
    assert decode_queries.shape[2] == 1 and kept_blocks.shape[2] == 1
    at, row = {}, ctx_local
    sizes = (
        ("values", BLOCK_POSITIONS),
        ("queries", round_up(steps * local_heads, 16)),
        ("tail_k", tail_len),
        ("tail_v", tail_len),
        ("notes", NOTE_ROWS),
    )
    for name, size in sizes:
        at[name] = row
        row += size
    layout = {
        "dims": (ctx_local, steps, local_heads, group_size, block_total, tail_len),
        "at": at,
        "scale": 1.0 / math.sqrt(HEAD_DIMENSION),
        "ctx": ctx_count,
    }
    me = ctx_index.astype(jnp.int32).reshape(1)
    group = grp_index.astype(jnp.int32).reshape(1)

    part_rows = win_rows // 2
    core = ctx_index % 2
    order = list(range(grp_count - 1, 0, -1))
    slices = pl.pallas_call(
        functools.partial(fetch_kernel, order, depth),
        out_shape=[pltpu.VMEM((part_rows, depth), jnp.bfloat16)] * len(order),
        in_specs=[smem(), smem(), far()],
        out_specs=[vmem()] * len(order),
        scratch_shapes=[pltpu.SemaphoreType.DMA((len(order),))],
        compiler_params=room(4),
    )(me, group, *away(states))
    fetched = {mask: swap(cell, "grp", mask) for mask, cell in zip(order, slices)}

    payload = pl.pallas_call(
        functools.partial(payload_kernel, layout),
        out_shape=[pltpu.VMEM((row, HEAD_DIMENSION), jnp.bfloat16)] * ctx_count,
        in_specs=[smem()] * 4 + [far()] * 2 + [vmem()] + [far()] * 2,
        out_specs=[vmem()] * ctx_count,
        scratch_shapes=[pltpu.SemaphoreType.DMA((ctx_count, 4))],
        compiler_params=room(8),
    )(
        me,
        kept_blocks.reshape(KEY_HEADS),
        retained_block_count.reshape(KEY_HEADS),
        row_lengths.reshape(1),
        *away(
            cache_keys[0],
            cache_values[0],
            decode_queries.reshape(steps, head_total * HEAD_DIMENSION),
            tail_keys[0, 0],
            tail_values[0, 0],
        ),
    )
    pieces = [payload[0]] + [swap(payload[m], "ctx", m) for m in range(1, ctx_count)]

    backs = []
    for mask in range(1, grp_count):
        mine = fetched[mask]
        other = swap(mine, "ctx", 1)
        both = jnp.where(
            core == 0,
            jnp.concatenate([mine, other], axis=0),
            jnp.concatenate([other, mine], axis=0),
        )
        partial = jnp.dot(both, query_weight, preferred_element_type=jnp.float32)
        backs.append(swap(partial.astype(jnp.float16), "grp", mask))
    own = lax.dynamic_slice(states, (0, grp_index * depth), (win_rows, depth))
    own, _ = lax.optimization_barrier((own, both))
    projected = jnp.dot(own, query_weight, preferred_element_type=jnp.float32)
    for back in backs:
        projected = projected + back.astype(jnp.float32)

    decoded = pl.pallas_call(
        functools.partial(decode_kernel, layout),
        out_shape=jax.ShapeDtypeStruct((ctx_count, steps, local_cols), jnp.bfloat16),
        in_specs=[smem()] + [vmem()] * ctx_count,
        out_specs=vmem(),
        compiler_params=room(8 + 24 * total_ctx // 16384),
    )(me, *near(*pieces))
    decoded = lax.all_to_all(decoded, "ctx", split_axis=0, concat_axis=0, tiled=True)
    decoded = decoded.transpose(1, 0, 2).reshape(steps, head_total * HEAD_DIMENSION)
    decode_out = decoded.reshape(1, steps, 1, head_total * HEAD_DIMENSION)

    positions = (jnp.arange(win_rows) + (total_ctx - win_rows)).astype(jnp.float32)
    cosine, sine = rotary_table(positions, HEAD_DIMENSION)
    cosine = jnp.concatenate([cosine, cosine], axis=1)
    sine = jnp.concatenate([-sine, sine], axis=1)
    pooled = pl.pallas_call(
        functools.partial(votes_kernel, layout),
        out_shape=jax.ShapeDtypeStruct((ctx_count, 1, ctx_local), jnp.float32),
        in_specs=[smem()] + [vmem()] * (3 + ctx_count) + [far()],
        out_specs=vmem(),
        compiler_params=room(20),
        scratch_shapes=[
            pltpu.VMEM((win_rows * local_heads, HEAD_DIMENSION), jnp.bfloat16),
            pltpu.VMEM((win_rows * local_heads, total_ctx), jnp.float32),
            pltpu.VMEM((win_rows * local_heads, LANES), jnp.float32),
            pltpu.VMEM((1, total_ctx + 2 * LANES), jnp.float32),
        ],
    )(me, *near(projected, cosine, sine, *pieces), *away(decoded))
    shares = lax.all_to_all(pooled, "ctx", split_axis=0, concat_axis=0, tiled=True)
    shares = shares.reshape(KEY_HEADS, sharers, ctx_local)
    pooled_votes = (shares[:, 0] if sharers == 1 else jnp.sum(shares, axis=1))[None]
    return (pooled_votes, decode_out)


def solution(mesh):
    placed = (
        P("grp", None, None),
        P("grp", "ctx"),
        P("grp", "ctx", None),
        P("grp", "ctx", None),
        P("grp", None, "ctx"),
        P("grp", None, "ctx"),
        P("grp", None, "ctx", None),
        P("grp", "ctx", None, None),
        P("grp", "ctx", None, None),
        P("grp", "ctx"),
    )

    return jax.shard_map(
        on_device,
        mesh=mesh,
        in_specs=placed,
        out_specs=(P("grp", None, "ctx"), P("grp", None, "ctx", None)),
        check_vma=False,
    )
```

```python
import functools
import math

import jax
import jax.numpy as jnp
from jax import lax
from jax.experimental import pallas as pl
from jax.experimental.pallas import tpu as pltpu
from jax.sharding import PartitionSpec as P


KEY_HEADS = 8
HEAD_DIMENSION = 128
BLOCK_POSITIONS = 128
POOL = 7
LANES = 128
NOTE_ROWS = 16


def rotary_table(positions, head_size):
    exponent = jnp.arange(0, head_size, 2).astype(jnp.float32) / head_size
    inverse = jnp.power(jnp.float32(500000.0), -exponent)
    wavelength = 2.0 * math.pi / inverse
    smooth = (8192.0 / wavelength - 1.0) / 3.0
    blended = (1.0 - smooth) * inverse / 8.0 + smooth * inverse
    adjusted = jnp.where(
        wavelength > 8192.0, inverse / 8.0, jnp.where(wavelength < 2048.0, inverse, blended)
    )
    angles = positions[:, None] * adjusted[None, :]
    return (jnp.cos(angles), jnp.sin(angles))


def swap(value, axis, mask):
    count = lax.axis_size(axis)
    return lax.ppermute(value, axis, [(i, i ^ mask) for i in range(count)])


def vmem():
    return pl.BlockSpec(memory_space=pltpu.VMEM)


def far():
    return pl.BlockSpec(memory_space=pltpu.HBM)


def smem():
    return pl.BlockSpec(memory_space=pltpu.SMEM)


def near(*arrays):
    return [pltpu.with_memory_space_constraint(a, pltpu.VMEM) for a in arrays]


def away(*arrays):
    return [pltpu.with_memory_space_constraint(a, pltpu.HBM) for a in arrays]


def room(mebibytes):
    return pltpu.CompilerParams(vmem_limit_bytes=mebibytes * 1024 * 1024)


def round_up(value, step):
    return (value + step - 1) // step * step


def dot_t(left, right):
    return lax.dot_general(
        left, right, (((1,), (1,)), ((), ())), preferred_element_type=jnp.float32
    )


def dot_exact(left, right):
    total = None
    for _ in range(3):
        part = left.astype(jnp.bfloat16)
        left = left - part.astype(jnp.float32)
        term = jnp.dot(part, right, preferred_element_type=jnp.float32)
        total = term if total is None else total + term
    return total


def fetch_kernel(order, depth, me_ref, group_ref, states_ref, *refs):
    outs, sems = refs[:-1], refs[-1]
    part_rows = outs[0].shape[0]
    start = pl.multiple_of(lax.rem(me_ref[0], 2) * part_rows, part_rows)
    copies = []
    for i, mask in enumerate(order):
        columns = pl.ds(pl.multiple_of((group_ref[0] ^ mask) * depth, LANES), depth)
        source = states_ref.at[pl.ds(start, part_rows), columns]
        copies.append(pltpu.make_async_copy(source, outs[i], sems.at[i]))
    for copy in copies:
        copy.start()
    for copy in copies:
        copy.wait()


def payload_kernel(
    layout, me_ref, group_ref, blocks_ref, counts_ref, lengths_ref, keys_ref, values_ref,
    query_ref, tail_k_ref, tail_v_ref, states_ref, *refs
):
    ctx_local, steps, local_heads, group_size, block_total, tail_len = layout["dims"]
    at = layout["at"]
    out_refs, own_ref, sems, own_sems = refs[:-3], refs[-3], refs[-2], refs[-1]
    me = me_ref[0]
    lane = lax.broadcasted_iota(jnp.int32, (NOTE_ROWS, LANES), 1)
    copies = []
    for mask, out in enumerate(out_refs):
        head = (me ^ mask) * local_heads // group_size
        columns = pl.ds(pl.multiple_of(head * HEAD_DIMENSION, HEAD_DIMENSION), HEAD_DIMENSION)
        block = jnp.clip(blocks_ref[head] - me * block_total, 0, block_total - 1)
        rows = pl.ds(pl.multiple_of(block * BLOCK_POSITIONS, BLOCK_POSITIONS), BLOCK_POSITIONS)
        moves = (
            (keys_ref.at[:, columns], 0, ctx_local),
            (values_ref.at[rows, columns], at["values"], BLOCK_POSITIONS),
            (tail_k_ref.at[:, columns], at["tail_k"], tail_len),
            (tail_v_ref.at[:, columns], at["tail_v"], tail_len),
        )
        for i, (source, start, size) in enumerate(moves):
            target = out.at[pl.ds(start, size), :]
            copies.append(pltpu.make_async_copy(source, target, sems.at[mask, i]))
            copies[-1].start()
    win, depth = own_ref.shape
    half = win // 2
    columns = pl.ds(pl.multiple_of(group_ref[0] * depth, LANES), depth)
    for i in range(2):
        start = pl.multiple_of((lax.rem(me, 2) ^ i) * half, half)
        source = states_ref.at[pl.ds(start, half), columns]
        copies.append(
            pltpu.make_async_copy(source, own_ref.at[pl.ds(i * half, half), :], own_sems.at[i])
        )
        copies[-1].start()
    for mask, out in enumerate(out_refs):
        dest = me ^ mask
        head = dest * local_heads // group_size
        block = jnp.clip(blocks_ref[head] - me * block_total, 0, block_total - 1)
        parts = []
        for g in range(local_heads):
            start = (dest * local_heads + g) * HEAD_DIMENSION
            cols = pl.ds(pl.multiple_of(start, HEAD_DIMENSION), HEAD_DIMENSION)
            parts.append(query_ref[:, cols].astype(jnp.float32))
        queries = jnp.concatenate(parts, axis=0)
        pad = at["tail_k"] - at["queries"] - steps * local_heads
        if pad:
            queries = jnp.concatenate(
                [queries, jnp.zeros((pad, HEAD_DIMENSION), jnp.float32)], axis=0
            )
        out[at["queries"] : at["tail_k"], :] = queries.astype(jnp.bfloat16)
        count = counts_ref[head].astype(jnp.float32)
        notes = jnp.where(
            lane == 0,
            count,
            jnp.where(
                lane == 1,
                block.astype(jnp.float32),
                jnp.where(lane == 2, lengths_ref[0].astype(jnp.float32), 0.0),
            ),
        )
        out[at["notes"] : at["notes"] + NOTE_ROWS, :] = notes.astype(jnp.bfloat16)
    for copy in copies:
        copy.wait()


def decode_kernel(layout, me_ref, *refs):
    _, steps, local_heads, _, block_total, tail_len = layout["dims"]
    at = layout["at"]
    scale = layout["scale"]
    pieces, out_ref = refs[:-1], refs[-1]
    me = me_ref[0]
    span = steps * local_heads
    kept_k, kept_v, queries, bias, tails = [], [], [], [], []
    for piece in pieces:
        notes = piece[at["notes"] : at["notes"] + NOTE_ROWS, :].astype(jnp.float32)
        block = notes[0:1, 1:2]
        bias.append(jnp.where(notes[0:1, 0:1] > 0.5, 0.0, -1e30))
        chosen = None
        for b in range(block_total):
            cell = piece[b * BLOCK_POSITIONS : (b + 1) * BLOCK_POSITIONS, :].astype(jnp.float32)
            term = cell * jnp.where(block == float(b), 1.0, 0.0)
            chosen = term if chosen is None else chosen + term
        kept_k.append(chosen.astype(jnp.bfloat16))
        kept_v.append(piece[at["values"] : at["values"] + BLOCK_POSITIONS, :])
        own = piece[at["queries"] : at["tail_k"], :]
        if at["tail_k"] - at["queries"] > span:
            own = own.astype(jnp.float32)[:span].astype(jnp.bfloat16)
        queries.append(own)
        score = dot_t(own, piece[at["tail_k"] : at["tail_k"] + tail_len, :]) * scale
        slot = lax.broadcasted_iota(jnp.int32, (span, tail_len), 1)
        step = lax.rem(lax.broadcasted_iota(jnp.int32, (span, tail_len), 0), steps)
        visible = (slot - step).astype(jnp.float32) < notes[0:1, 2:3]
        tails.append(jnp.where(visible, score, -1e30))
    every = jnp.concatenate(queries, axis=0)
    scores = [dot_t(every, k) * scale + b for k, b in zip(kept_k, bias)]
    peak = scores[0]
    for s in scores[1:]:
        peak = jnp.maximum(peak, s)
    peak = jnp.max(peak, axis=1, keepdims=True)
    tail_peak = jnp.concatenate([jnp.max(t, axis=1, keepdims=True) for t in tails], axis=0)
    peak = jnp.maximum(peak, tail_peak)
    weights = [jnp.exp(s - peak) for s in scores]
    total = weights[0]
    for w in weights[1:]:
        total = total + w
    total = jnp.sum(total, axis=1, keepdims=True)
    numerator = dot_exact(jnp.concatenate(weights, axis=1), jnp.concatenate(kept_v, axis=0))
    for mask, piece in enumerate(pieces):
        lo = mask * span
        weight = jnp.exp(tails[mask] - peak[lo : lo + span])
        part = dot_exact(weight, piece[at["tail_v"] : at["tail_v"] + tail_len, :])
        top = numerator[lo : lo + span] + part
        bottom = total[lo : lo + span] + jnp.sum(weight, axis=1, keepdims=True)
        result = top / bottom
        dest = me ^ mask
        for g in range(local_heads):
            out_ref[dest, :, g * HEAD_DIMENSION : (g + 1) * HEAD_DIMENSION] = result[
                g * steps : (g + 1) * steps
            ].astype(jnp.bfloat16)


def votes_kernel(layout, me_ref, projected_ref, cos_ref, sin_ref, *refs):
    ctx_local, _, local_heads, group_size, _, _ = layout["dims"]
    count = layout["ctx"]
    win = projected_ref.shape[0]
    pieces, out_ref = refs[:count], refs[count]
    query_ref, score_ref, peak_ref, sums_ref = refs[count + 1 :]
    me = me_ref[0]
    total_ctx = ctx_local * count
    start_pos = total_ctx - win
    folded = layout["scale"] * math.log2(math.e)
    rows = win * local_heads
    width = 2 * LANES
    half = HEAD_DIMENSION // 2
    parts = [pl.ds(pl.multiple_of((lax.rem(me, 2) ^ i) * (win // 2), win // 2), win // 2) for i in (0, 1)]
    cosine = jnp.concatenate([cos_ref[part, :] for part in parts], axis=0)
    sine = jnp.concatenate([sin_ref[part, :] for part in parts], axis=0)
    for g in range(local_heads):
        x = projected_ref[:, g * HEAD_DIMENSION : (g + 1) * HEAD_DIMENSION]
        turned = jnp.concatenate([x[:, half:], x[:, :half]], axis=1)
        turned = x * cosine + turned * sine
        query_ref[g * win : (g + 1) * win, :] = turned.astype(jnp.bfloat16)
    window_row = lax.broadcasted_iota(jnp.int32, (win, LANES), 0) + lax.rem(me, 2) * (win // 2)
    window_row = jnp.where(window_row >= win, window_row - win, window_row)
    offset = lax.broadcasted_iota(jnp.int32, (win, LANES), 1) - window_row
    for mask, piece in enumerate(pieces):
        base = (me ^ mask) * ctx_local
        for c in range(0, ctx_local, width):
            score = dot_t(query_ref[...], piece[c : c + width, :])
            if c + width == ctx_local:
                seen = offset <= start_pos - base - (ctx_local - LANES)
                last = score[:, LANES:].reshape(local_heads, win, LANES)
                last = jnp.where(seen[None], last, -1e30).reshape(rows, LANES)
                score = jnp.concatenate([score[:, :LANES], last], axis=1)
            score_ref[:, pl.ds(pl.multiple_of(base + c, LANES), width)] = score
            top = jnp.maximum(score[:, :LANES], score[:, LANES:])
            first = mask == 0 and c == 0
            peak_ref[...] = top if first else jnp.maximum(peak_ref[...], top)
    votes = None
    for g in range(local_heads):
        at = slice(g * win, (g + 1) * win)
        peak = jnp.max(peak_ref[at, :], axis=1, keepdims=True) * folded
        weight = jnp.exp2(score_ref[at, :] * folded - peak)
        share = 1.0 / jnp.sum(weight, axis=1, keepdims=True)
        weight = weight * share
        cells = jnp.sum(weight.reshape(win // 8, 8, total_ctx), axis=0)
        votes = cells if votes is None else votes + cells
    row = jnp.sum(votes, axis=0, keepdims=True) * (total_ctx / (win * group_size))
    sums_ref[:, 0:LANES] = jnp.zeros((1, LANES), jnp.float32)
    sums_ref[:, LANES : LANES + total_ctx] = row
    sums_ref[:, LANES + total_ctx :] = jnp.zeros((1, LANES), jnp.float32)
    pooled = None
    for shift in range(POOL):
        start = LANES - (POOL - 1) // 2 + shift
        term = sums_ref[:, start : start + total_ctx]
        pooled = term if pooled is None else pooled + term
    pooled = pooled / POOL
    for c in range(count):
        out_ref[c] = pooled[:, c * ctx_local : (c + 1) * ctx_local]


def on_device(
    window_states,
    query_weight,
    cache_keys,
    cache_values,
    kept_blocks,
    retained_block_count,
    decode_queries,
    tail_keys,
    tail_values,
    row_lengths,
):
    ctx_count = lax.axis_size("ctx")
    grp_count = lax.axis_size("grp")
    ctx_index = lax.axis_index("ctx")
    grp_index = lax.axis_index("grp")
    states = window_states[0]
    win_rows = states.shape[0]
    depth, local_cols = query_weight.shape
    local_heads = local_cols // HEAD_DIMENSION
    head_total = local_heads * ctx_count
    group_size = head_total // KEY_HEADS
    sharers = group_size // local_heads
    ctx_local = cache_keys.shape[1]
    total_ctx = ctx_local * ctx_count
    steps = decode_queries.shape[1]
    tail_len = tail_keys.shape[2]
    block_total = ctx_local // BLOCK_POSITIONS
    assert decode_queries.shape[2] == 1 and kept_blocks.shape[2] == 1
    at, row = {}, ctx_local
    sizes = (
        ("values", BLOCK_POSITIONS),
        ("queries", round_up(steps * local_heads, 16)),
        ("tail_k", tail_len),
        ("tail_v", tail_len),
        ("notes", NOTE_ROWS),
    )
    for name, size in sizes:
        at[name] = row
        row += size
    layout = {
        "dims": (ctx_local, steps, local_heads, group_size, block_total, tail_len),
        "at": at,
        "scale": 1.0 / math.sqrt(HEAD_DIMENSION),
        "ctx": ctx_count,
    }
    me = ctx_index.astype(jnp.int32).reshape(1)
    group = grp_index.astype(jnp.int32).reshape(1)

    part_rows = win_rows // 2
    order = list(range(grp_count - 1, 0, -1))
    slices = pl.pallas_call(
        functools.partial(fetch_kernel, order, depth),
        out_shape=[pltpu.VMEM((part_rows, depth), jnp.bfloat16)] * len(order),
        in_specs=[smem(), smem(), far()],
        out_specs=[vmem()] * len(order),
        scratch_shapes=[pltpu.SemaphoreType.DMA((len(order),))],
        compiler_params=room(4),
    )(me, group, *away(states))
    fetched = {mask: swap(cell, "grp", mask) for mask, cell in zip(order, slices)}

    *payload, own = pl.pallas_call(
        functools.partial(payload_kernel, layout),
        out_shape=[pltpu.VMEM((row, HEAD_DIMENSION), jnp.bfloat16)] * ctx_count
        + [pltpu.VMEM((win_rows, depth), jnp.bfloat16)],
        in_specs=[smem()] * 5 + [far()] * 2 + [vmem()] + [far()] * 3,
        out_specs=[vmem()] * (ctx_count + 1),
        scratch_shapes=[
            pltpu.SemaphoreType.DMA((ctx_count, 4)),
            pltpu.SemaphoreType.DMA((2,)),
        ],
        compiler_params=room(8),
    )(
        me,
        group,
        *away(kept_blocks.reshape(KEY_HEADS), retained_block_count.reshape(KEY_HEADS)),
        row_lengths.reshape(1),
        *away(
            cache_keys[0],
            cache_values[0],
            decode_queries.reshape(steps, head_total * HEAD_DIMENSION),
            tail_keys[0, 0],
            tail_values[0, 0],
            states,
        ),
    )
    pieces = [payload[0]] + [swap(payload[m], "ctx", m) for m in range(1, ctx_count)]

    backs = []
    for mask in range(1, grp_count):
        mine = fetched[mask]
        other = swap(mine, "ctx", 1)
        both = jnp.concatenate([mine, other], axis=0)
        partial = jnp.dot(both, query_weight, preferred_element_type=jnp.float32)
        backs.append(swap(partial.astype(jnp.float16), "grp", mask))
    projected = jnp.dot(own, query_weight, preferred_element_type=jnp.float32)
    for back in backs:
        projected = projected + back.astype(jnp.float32)

    decoded = pl.pallas_call(
        functools.partial(decode_kernel, layout),
        out_shape=jax.ShapeDtypeStruct((ctx_count, steps, local_cols), jnp.bfloat16),
        in_specs=[smem()] + [vmem()] * ctx_count,
        out_specs=vmem(),
        compiler_params=room(8 + 24 * total_ctx // 16384),
    )(me, *near(*pieces))
    decoded = lax.all_to_all(decoded, "ctx", split_axis=0, concat_axis=0, tiled=True)
    decoded = decoded.transpose(1, 0, 2).reshape(steps, head_total * HEAD_DIMENSION)
    decode_out = decoded.reshape(1, steps, 1, head_total * HEAD_DIMENSION)

    positions = (jnp.arange(win_rows) + (total_ctx - win_rows)).astype(jnp.float32)
    cosine, sine = rotary_table(positions, HEAD_DIMENSION)
    cosine = jnp.concatenate([cosine, cosine], axis=1)
    sine = jnp.concatenate([-sine, sine], axis=1)
    pooled = pl.pallas_call(
        functools.partial(votes_kernel, layout),
        out_shape=jax.ShapeDtypeStruct((ctx_count, 1, ctx_local), jnp.float32),
        in_specs=[smem()] + [vmem()] * (3 + ctx_count),
        out_specs=vmem(),
        compiler_params=room(20),
        scratch_shapes=[
            pltpu.VMEM((win_rows * local_heads, HEAD_DIMENSION), jnp.bfloat16),
            pltpu.VMEM((win_rows * local_heads, total_ctx), jnp.float32),
            pltpu.VMEM((win_rows * local_heads, LANES), jnp.float32),
            pltpu.VMEM((1, total_ctx + 2 * LANES), jnp.float32),
        ],
    )(me, *near(projected, cosine, sine, *pieces))
    shares = lax.all_to_all(pooled, "ctx", split_axis=0, concat_axis=0, tiled=True)
    shares = shares.reshape(KEY_HEADS, sharers, ctx_local)
    pooled_votes = (shares[:, 0] if sharers == 1 else jnp.sum(shares, axis=1))[None]
    return (pooled_votes, decode_out)


def solution(mesh):
    placed = (
        P("grp", None, None),
        P("grp", "ctx"),
        P("grp", "ctx", None),
        P("grp", "ctx", None),
        P("grp", None, "ctx"),
        P("grp", None, "ctx"),
        P("grp", None, "ctx", None),
        P("grp", "ctx", None, None),
        P("grp", "ctx", None, None),
        P("grp", "ctx"),
    )

    return jax.shard_map(
        on_device,
        mesh=mesh,
        in_specs=placed,
        out_specs=(P("grp", None, "ctx"), P("grp", None, "ctx", None)),
        check_vma=False,
    )
```
